32 devices in a mesh: grp: 2 (over x), ctx: 8 (over z, y), shd: 2 (over core).
Axes of the slice: x: 2, y: 2, z: 4, core: 2. Of those that a mesh axis runs over, the one named last changes fastest.
Arguments:
- train_values: bfloat16 [2, 2048, 8192], P('grp', 'ctx', 'shd'), may hold values from -6 to 6
- train_gates: bfloat16 [2, 2048, 8192], P('grp', 'ctx', 'shd'), may hold values from -6 to 6
- train_writes: bfloat16 [2, 2048, 1024], P('grp', 'ctx', 'shd'), may hold values from -6 to 6
- train_reads: bfloat16 [2, 2048, 1024], P('grp', 'ctx', 'shd'), may hold values from -6 to 6
- train_steps: float32 [2, 2048, 128], P('grp', 'ctx', 'shd'), may hold values from -4 to 4
- out_cotangent: bfloat16 [2, 2048, 8192], P('grp', 'ctx', 'shd'), may hold values from -6 to 6
- head_params: float32 [3, 128], P(None, 'shd'), may hold values from -10.5 to 1.5, as said below
- norm_gain: float32 [8192], P('shd'), may hold values from 0.5 to 1.5
- slow_heads: float32 [3, 128], P(None, 'shd'), may hold values from -10.5 to 1.5, as said below
- slow_gain: float32 [8192], P('shd'), may hold values from 0.5 to 1.5
- roll_state: bfloat16 [32, 128, 64, 128], P(('grp', 'ctx'), 'shd'), may hold values from -6 to 6
- roll_values: bfloat16 [32, 4, 8192], P(('grp', 'ctx'), None, 'shd'), may hold values from -6 to 6
- roll_gates: bfloat16 [32, 4, 8192], P(('grp', 'ctx'), None, 'shd'), may hold values from -6 to 6
- roll_writes: bfloat16 [32, 4, 1024], P(('grp', 'ctx'), None, 'shd'), may hold values from -6 to 6
- roll_reads: bfloat16 [32, 4, 1024], P(('grp', 'ctx'), None, 'shd'), may hold values from -6 to 6
- roll_steps: float32 [32, 4, 128], P(('grp', 'ctx'), None, 'shd'), may hold values from -4 to 4
- roll_lengths: int32 [32], P(('grp', 'ctx')), may hold values from 1 to 4
Outputs:
- seq_out: bfloat16 [2, 2048, 8192], P('grp', 'ctx', 'shd')
- gradient_heads: float32 [3, 128], P(None, 'shd')
- gradient_gain: float32 [8192], P('shd')
- blend_heads: float32 [3, 128], P(None, 'shd')
- blend_gain: float32 [8192], P('shd')
- roll_out: bfloat16 [32, 4, 8192], P(('grp', 'ctx'), None, 'shd')
- roll_final: float32 [32, 128, 64, 128], P(('grp', 'ctx'), 'shd')
The draws below stay inside these ranges and needn't reach their ends.
Inputs may be any that keep to these rules, and one draw needn't show every extreme that they name: `head_params`: row 0 is the natural logarithm of each head's decay rate, row 1 the bias added to the raw step before softplus, row 2 the skip coefficient. `slow_heads`: rows as in head_params.
All inputs are finite; a program needn't handle non-finite values.
Results may differ from the reference program's by a relative error of at most 0.0017.
Values sent between devices are 32-bit elements; how exact they have to be, the bound alone decides.
A program may use at most 128 MiB of HBM per device.

```python
import math
import jax
import jax.numpy as jnp
from jax import lax

HEADS = 128
HEAD_DIM = 64
STATE = 128
GROUPS = 8
INNER = 8192
BLOCK = 256
LENGTH = 2048
SEQS = 2
ROWS = 32
STEPS = 4


def head_law(key):
    slow_pick = jax.random.bernoulli(jax.random.fold_in(key, 1), 0.5, (HEADS,))
    slow_rates = jax.random.uniform(jax.random.fold_in(key, 2), (HEADS,), jnp.float32, math.log(3e-05), math.log(0.0003))
    fast_rates = jax.random.uniform(jax.random.fold_in(key, 3), (HEADS,), jnp.float32, math.log(0.003), math.log(0.05))
    rate_log = jnp.where(slow_pick, slow_rates, fast_rates)
    step_bias = jax.random.uniform(jax.random.fold_in(key, 4), (HEADS,), jnp.float32, -2.0, 1.0)
    skip_gain = jax.random.uniform(jax.random.fold_in(key, 5), (HEADS,), jnp.float32, 0.2, 1.5)
    return jnp.stack([rate_log, step_bias, skip_gain]).astype(jnp.float32)


def draw_head_params(key, part):
    return head_law(jax.random.fold_in(key, 5))


def draw_slow_heads(key, part):
    return head_law(jax.random.fold_in(key, 11))


def set_ends(drawn, rng, least, top_value):
    shape = drawn.shape
    index_at = [jax.random.randint(jax.random.fold_in(rng, axis), (), 0, shape[axis]) for axis in range(len(shape))]
    drawn = drawn.at[tuple(index_at)].set(least)
    longest = shape.index(max(shape))
    index_at[longest] = (index_at[longest] + 1) % shape[longest]
    return drawn.at[tuple(index_at)].set(top_value)


def steps_of(rng, dims, pieces, low, largest):
    factor_of, own = 1.0, jax.random.fold_in(rng, 6)
    for axis_at, blocks in pieces:
        heights = jnp.exp(jax.random.uniform(jax.random.fold_in(own, axis_at), (blocks,), jnp.float32, low / len(pieces), largest / len(pieces)))
        factor_of = factor_of * jnp.repeat(heights, dims[axis_at] // blocks).reshape([-1 if axis == axis_at else 1 for axis in range(len(dims))])
    return factor_of


def gaussian(key, dims, width, bound, split=(), kind=jnp.bfloat16):
    entries = width * jax.random.normal(key, dims, jnp.float32)
    if split:
        entries = entries * steps_of(key, dims, split, -0.22, 0.18)
    return jnp.clip(entries, -bound, bound).astype(kind)


def setup_inputs(seed: int = 0) -> dict:
    splits = jax.random.split(jax.random.key(seed), 18)
    return {
        "train_values": gaussian(splits[0], (SEQS, LENGTH, INNER), 1.0, 6.0, ((0, 2), (1, 8), (2, 2))),
        "train_gates": gaussian(splits[1], (SEQS, LENGTH, INNER), 1.0, 6.0, ((0, 2), (1, 8), (2, 2))),
        "train_writes": gaussian(splits[2], (SEQS, LENGTH, GROUPS * STATE), 1.0, 6.0, ((0, 2), (1, 8), (2, 2))),
        "train_reads": gaussian(splits[3], (SEQS, LENGTH, GROUPS * STATE), 1.0, 6.0, ((0, 2), (1, 8), (2, 2))),
        "train_steps": gaussian(splits[4], (SEQS, LENGTH, HEADS), 1.0, 4.0, ((0, 2), (1, 8), (2, 2)), jnp.float32),
        "out_cotangent": gaussian(splits[5], (SEQS, LENGTH, INNER), 1.0, 6.0, ((0, 2), (1, 8), (2, 2))),
        "head_params": draw_head_params(jax.random.fold_in(splits[17], 71), 0),
        "norm_gain": jnp.clip(1.0 + 0.1 * jax.random.normal(splits[7], (INNER,), jnp.float32), 0.5, 1.5),
        "slow_heads": draw_slow_heads(jax.random.fold_in(splits[17], 71), 0),
        "slow_gain": jnp.clip(1.0 + 0.1 * jax.random.normal(splits[9], (INNER,), jnp.float32), 0.5, 1.5),
        "roll_state": gaussian(splits[10], (ROWS, HEADS, HEAD_DIM, STATE), 1.0, 6.0, ((0, 16), (1, 2))),
        "roll_values": gaussian(splits[11], (ROWS, STEPS, INNER), 1.0, 6.0, ((0, 16), (2, 2))),
        "roll_gates": gaussian(splits[12], (ROWS, STEPS, INNER), 1.0, 6.0, ((0, 16), (2, 2))),
        "roll_writes": gaussian(splits[13], (ROWS, STEPS, GROUPS * STATE), 1.0, 6.0, ((0, 16), (2, 2))),
        "roll_reads": gaussian(splits[14], (ROWS, STEPS, GROUPS * STATE), 1.0, 6.0, ((0, 16), (2, 2))),
        "roll_steps": gaussian(splits[15], (ROWS, STEPS, HEADS), 1.0, 4.0, ((0, 16), (2, 2)), jnp.float32),
        "roll_lengths": set_ends(jax.random.randint(splits[16], (ROWS,), 1, STEPS + 1), jax.random.fold_in(splits[16], 1), 1, STEPS).astype(jnp.int32),
    }


HIGHEST = lax.Precision.HIGHEST
EPSILON = 1e-05
KEEP_SHARE = 0.75
STEP_RATE = 0.001

def block_terms(carried_in, block_data):
    state_now, offset = carried_in
    values, writes, reads, step_sizes, log_decay = block_data
    cumulative = jnp.cumsum(log_decay, axis=0)
    length = log_decay.shape[0]
    rows_iota = lax.broadcasted_iota(jnp.int32, (length, length), 0)
    cols_iota = lax.broadcasted_iota(jnp.int32, (length, length), 1)
    causal = (rows_iota >= cols_iota)[:, :, None]
    spread = jnp.where(causal, cumulative[:, None, :] - cumulative[None, :, :], 0.0)
    weights = jnp.where(causal, jnp.exp(spread), 0.0) * step_sizes[None, :, :]
    scores = jnp.einsum('thn,shn->tsh', reads, writes, precision=HIGHEST)
    inside = jnp.einsum('tsh,shp->thp', scores * weights, values, precision=HIGHEST)
    carried = jnp.exp(cumulative)[:, :, None] * jnp.einsum('thn,hpn->thp', reads, state_now, precision=HIGHEST)
    last_sum = cumulative[-1]
    tail_weight = jnp.exp(last_sum[None, :] - cumulative) * step_sizes
    fresh = jnp.einsum('sh,shp,shn->hpn', tail_weight, values, writes, precision=HIGHEST)
    new_state = jnp.exp(last_sum)[:, None, None] * state_now + fresh
    return ((new_state, offset + last_sum), (inside + carried, offset + cumulative))

def run_blocks(params, values, writes, reads, raw_steps, start_state):
    rate_log, step_bias, skip_gain = params
    step_sizes = jax.nn.softplus(raw_steps + step_bias)
    log_decay = -jnp.exp(rate_log) * step_sizes
    tokens, heads, head_width = values.shape
    block_count = tokens // BLOCK
    blocks = (values.reshape(block_count, BLOCK, heads, head_width), writes.reshape(block_count, BLOCK, heads, -1), reads.reshape(block_count, BLOCK, heads, -1), step_sizes.reshape(block_count, BLOCK, heads), log_decay.reshape(block_count, BLOCK, heads))
    offset = jnp.zeros((heads,), jnp.float32)
    (final, unused), (outputs, decay_sum) = lax.scan(jax.checkpoint(block_terms), (start_state, offset), blocks)
    local_out = outputs.reshape(tokens, heads, head_width) + skip_gain[:, None] * values
    return (local_out, final, decay_sum.reshape(tokens, heads))

def expand_groups(packed):
    grouped = packed.astype(jnp.float32).reshape(packed.shape[:-1] + (GROUPS, STATE))
    return jnp.repeat(grouped, HEADS // GROUPS, axis=-2)

def reference(train_values, train_gates, train_writes, train_reads, train_steps, out_cotangent, head_params, norm_gain, slow_heads, slow_gain, roll_state, roll_values, roll_gates, roll_writes, roll_reads, roll_steps, roll_lengths):
    params = (head_params[0], head_params[1], head_params[2])
    empty = jnp.zeros((HEADS, HEAD_DIM, STATE), jnp.float32)

    def train_loss(weights, gain):
        outputs = []
        loss_total = jnp.zeros((), jnp.float32)
        for seq_index in range(SEQS):
            values = train_values[seq_index].astype(jnp.float32).reshape(LENGTH, HEADS, HEAD_DIM)
            writes = expand_groups(train_writes[seq_index])
            reads = expand_groups(train_reads[seq_index])
            mixed_out, final, decay_sum = run_blocks(weights, values, writes, reads, train_steps[seq_index], empty)
            gated_out = mixed_out.reshape(LENGTH, INNER) * jax.nn.silu(train_gates[seq_index].astype(jnp.float32))
            inverse = lax.rsqrt(lax.optimization_barrier(jnp.mean(gated_out * gated_out, axis=1, keepdims=True)) + EPSILON)
            normed = gated_out * inverse * gain
            loss_total = loss_total + jnp.sum(normed * out_cotangent[seq_index].astype(jnp.float32))
            outputs.append(normed)
        return (loss_total, jnp.stack(outputs))
    loss_total, pullback, trained = jax.vjp(train_loss, params, norm_gain, has_aux=True)
    head_slope, gain_slope = pullback(jnp.ones_like(loss_total))
    gradient_heads = jnp.stack(list(head_slope))
    blend_heads = KEEP_SHARE * slow_heads + (1.0 - KEEP_SHARE) * (head_params - STEP_RATE * gradient_heads)
    blend_gain = KEEP_SHARE * slow_gain + (1.0 - KEEP_SHARE) * (norm_gain - STEP_RATE * gain_slope)
    decay_rate = jnp.exp(blend_heads[0])
    step_bias = blend_heads[1]
    skip_gain = blend_heads[2]

    def roll_row(row_items):
        start_state, row_values, row_gates, row_writes, row_reads, row_steps, row_length = row_items
        carried = start_state.astype(jnp.float32)
        outputs = []
        for turn_index in range(STEPS):
            active = row_length > turn_index
            step_sizes = jax.nn.softplus(row_steps[turn_index] + step_bias)
            decay_now = jnp.exp(-decay_rate * step_sizes)
            values = row_values[turn_index].astype(jnp.float32).reshape(HEADS, HEAD_DIM)
            writes = expand_groups(row_writes[turn_index])
            reads = expand_groups(row_reads[turn_index])
            update = decay_now[:, None, None] * carried + (step_sizes[:, None] * values)[:, :, None] * writes[:, None, :]
            carried = jnp.where(active, update, carried)
            read_out = jnp.einsum('hn,hpn->hp', reads, carried, precision=HIGHEST) + skip_gain[:, None] * values
            gated_out = read_out.reshape(INNER) * jax.nn.silu(row_gates[turn_index].astype(jnp.float32))
            inverse = lax.rsqrt(jnp.mean(gated_out * gated_out) + EPSILON)
            outputs.append(jnp.where(active, gated_out * inverse * blend_gain, 0.0))
        return (jnp.stack(outputs).astype(jnp.bfloat16), carried)
    roll_out, roll_final = lax.map(roll_row, (roll_state, roll_values, roll_gates, roll_writes, roll_reads, roll_steps, roll_lengths))
    return (trained.astype(jnp.bfloat16), gradient_heads, gain_slope, blend_heads, blend_gain, roll_out, roll_final)
```

```python
import functools

import jax
import jax.numpy as jnp
from jax import lax
from jax.experimental import pallas as pl
from jax.experimental.pallas import tpu as pltpu
from jax.sharding import PartitionSpec as P

HEAD_DIM = 64
STATE = 128
STEPS = 4
LANES = 256

HIGHEST = lax.Precision.HIGHEST
MESH = pl.DeviceIdType.MESH
EPSILON = 1e-05
KEEP_SHARE = 0.75
STEP_RATE = 0.001
F32 = jnp.float32
BF16 = jnp.bfloat16


def expand_groups(packed, heads):
    groups = packed.shape[-1] // STATE
    grouped = packed.reshape(packed.shape[:-1] + (groups, STATE))
    return jnp.repeat(grouped, heads // groups, axis=-2)


def pieces(a, count):
    out = []
    for i in range(count):
        piece = a.astype(BF16)
        out.append(piece)
        if i + 1 < count:
            a = a - piece.astype(F32)
    return out


def mm(a, b, dims=(1, 0)):
    return lax.dot_general(
        a, b, (((dims[0],), (dims[1],)), ((), ())), preferred_element_type=F32
    )


def left(parts, b, dims=(1, 0)):
    total = mm(parts[-1], b, dims)
    for part in parts[-2::-1]:
        total = total + mm(part, b, dims)
    return total


def right(a, parts, dims=(1, 0)):
    total = mm(a, parts[-1], dims)
    for part in parts[-2::-1]:
        total = total + mm(a, part, dims)
    return total


def silu_of(gate):
    return gate / (1.0 + jnp.exp(-gate))


def trained(
    sizes,
    x_ref,
    gate_ref,
    b_ref,
    c_ref,
    cot_ref,
    dt_ref,
    dtt_ref,
    sig_ref,
    par_ref,
    part_ref,
    gain_ref,
    seq_ref,
    head_ref,
    total_ref,
    a_ref,
    at_ref,
    local_ref,
    state_ref,
    slope_ref,
    later_ref,
    mhi_ref,
    mlo_ref,
    mixed_ref,
    ghi_ref,
    glo_ref,
    q_ref,
    r_ref,
    skip_ref,
    end_ref,
    gsum_ref,
    ex_ref,
    exr_ref,
    gains_ref,
    hs_ref,
    heads_ref,
    fs_sem,
    fr_sem,
    bs_sem,
    br_sem,
    es_sem,
    er_sem,
    gs_sem,
    gr_sem,
    hs_sem,
    hr_sem,
):
    n_grp, n_ctx, n_shd = sizes
    tokens, inner_local = x_ref.shape
    heads = dt_ref.shape[1]
    groups = b_ref.shape[1] // STATE
    chunks = inner_local // LANES
    per_group = chunks // groups
    per_chunk = LANES // HEAD_DIM
    inner = inner_local * n_shd
    grp = lax.axis_index("grp")
    ctx = lax.axis_index("ctx")
    shd = lax.axis_index("shd")
    peers = n_grp * n_ctx
    me = grp * n_ctx + ctx

    barrier = pltpu.get_barrier_semaphore()
    for o in range(1, peers):
        other = lax.rem(me + o, peers)
        pl.semaphore_signal(
            barrier,
            inc=1,
            device_id={"grp": other // n_ctx, "ctx": lax.rem(other, n_ctx)},
            device_id_type=MESH,
        )
    for o in range(1, n_shd):
        pl.semaphore_signal(
            barrier, inc=1, device_id={"shd": lax.rem(shd + o, n_shd)}, device_id_type=MESH
        )

    row_t = lax.broadcasted_iota(jnp.int32, (tokens, tokens), 0)
    col_t = lax.broadcasted_iota(jnp.int32, (tokens, tokens), 1)
    causal = row_t >= col_t
    lower = jnp.where(causal, 1.0, 0.0).astype(BF16)
    upper = jnp.where(row_t <= col_t, 1.0, 0.0).astype(BF16)
    lane_head = lax.broadcasted_iota(jnp.int32, (tokens, LANES), 1) // HEAD_DIM
    head_row = lax.broadcasted_iota(jnp.int32, (heads, LANES), 0)
    head_lane = lax.broadcasted_iota(jnp.int32, (heads, LANES), 1) // HEAD_DIM

    rate = jnp.exp(par_ref[0:1, :])
    decay = -rate * dt_ref[...]
    a_ref[...] = right(lower, pieces(decay, 3))
    decay_t = -jnp.exp(part_ref[:, 0:1]) * dtt_ref[...]
    at_ref[...] = left(pieces(decay_t, 3), upper)

    def spread_of(c):
        return jnp.where(head_row == c * per_chunk + head_lane, 1.0, 0.0).astype(BF16)

    def lanes(c):
        return pl.ds(pl.multiple_of(c * LANES, LANES), LANES)

    def states(c):
        return pl.ds(pl.multiple_of(c // per_group * STATE, STATE), STATE)

    def expanded(c):
        spread = spread_of(c)
        a_c = left(pieces(a_ref[...], 3), spread)
        dt_c = left(pieces(dt_ref[...], 3), spread)
        return spread, a_c, dt_c

    def local_state(c, carry):
        spread, a_c, dt_c = expanded(c)
        weight = jnp.exp(a_c[tokens - 1 : tokens, :] - a_c) * dt_c
        fresh = weight * x_ref[:, lanes(c)].astype(F32)
        local_ref[:, lanes(c)] = right(b_ref[:, states(c)], pieces(fresh, 2), (0, 0))
        return carry

    lax.fori_loop(0, chunks, local_state, 0)

    @pl.when(ctx == 0)
    def _():
        state_ref[...] = jnp.zeros_like(state_ref)

    @pl.when(ctx == n_ctx - 1)
    def _():
        later_ref[...] = jnp.zeros_like(later_ref)

    pl.semaphore_wait(barrier, peers - 1 + n_shd - 1)

    def forward_copy(c):
        return pltpu.make_async_remote_copy(
            src_ref=local_ref.at[:, lanes(c)],
            dst_ref=state_ref.at[:, lanes(c)],
            send_sem=fs_sem.at[c],
            recv_sem=fr_sem.at[c],
            device_id={"ctx": lax.rem(ctx + 1, n_ctx)},
            device_id_type=MESH,
        )

    def backward_copy(c):
        return pltpu.make_async_remote_copy(
            src_ref=slope_ref.at[:, lanes(c)],
            dst_ref=later_ref.at[:, lanes(c)],
            send_sem=bs_sem.at[c],
            recv_sem=br_sem.at[c],
            device_id={"ctx": lax.rem(ctx + n_ctx - 1, n_ctx)},
            device_id_type=MESH,
        )

    ex_ref[...] = jnp.zeros_like(ex_ref)
    q_ref[...] = jnp.zeros_like(q_ref)
    r_ref[...] = jnp.zeros_like(r_ref)

    def fold(a):
        total = a[:, :128]
        for i in range(128, a.shape[1], 128):
            total = total + a[:, i : i + 128]
        return total

    def forward(c, carry):
        squares, products = carry
        spread, a_c, dt_c = expanded(c)

        @pl.when(ctx > 0)
        def _():
            forward_copy(c).wait_recv()
            local_ref[:, lanes(c)] = (
                jnp.exp(a_c[tokens - 1 : tokens, :]) * state_ref[:, lanes(c)]
                + local_ref[:, lanes(c)]
            )

        @pl.when(ctx < n_ctx - 1)
        def _():
            forward_copy(c).start()

        x_c = x_ref[:, lanes(c)]
        x_wide = x_c.astype(F32)
        scores = mm(c_ref[:, states(c)], b_ref[:, states(c)], (1, 1))
        read_in = right(c_ref[:, states(c)], pieces(state_ref[:, lanes(c)], 2))
        skip_c = left(pieces(par_ref[2:3, :] + jnp.zeros((8, heads), F32), 3), spread)[0:1]
        mixed = jnp.exp(a_c) * read_in + skip_c * x_wide
        for i in range(per_chunk):
            head = c * per_chunk + i
            gap = a_c[:, i * HEAD_DIM : i * HEAD_DIM + 1] - at_ref[pl.ds(head, 1), :]
            weight = jnp.exp(jnp.where(causal, gap, -1e30)) * dtt_ref[pl.ds(head, 1), :]
            both = pieces(scores * weight, 2)
            mhi_ref[head] = both[0]
            mlo_ref[head] = both[1]
            own = jnp.where(lane_head == i, x_wide, 0.0).astype(BF16)
            mixed = mixed + left(both, own)
        mixed_ref[:, lanes(c)] = mixed
        gated = mixed * silu_of(gate_ref[:, lanes(c)].astype(F32))
        weighted = cot_ref[:, lanes(c)].astype(F32) * gain_ref[:, lanes(c)]
        return (squares + fold(gated * gated), products + fold(weighted * gated))

    zero = jnp.zeros((tokens, 128), F32)
    squares, products = lax.fori_loop(0, chunks, forward, (zero, zero))
    lane = lax.broadcasted_iota(jnp.int32, (tokens, 128), 1)
    ex_ref[...] = jnp.where(
        lane < 64,
        jnp.sum(squares, axis=1, keepdims=True),
        jnp.sum(products, axis=1, keepdims=True),
    )
    copies = []
    for o in range(1, n_shd):
        copies.append(
            pltpu.make_async_remote_copy(
                src_ref=ex_ref,
                dst_ref=exr_ref.at[o - 1],
                send_sem=es_sem.at[o - 1],
                recv_sem=er_sem.at[o - 1],
                device_id={"shd": lax.rem(shd + o, n_shd)},
                device_id_type=MESH,
            )
        )
        copies[-1].start()
    joined = ex_ref[...]
    for o in range(1, n_shd):
        copies[o - 1].wait()
        joined = joined + exr_ref[o - 1]
    inverse = lax.rsqrt(joined[:, 0:1] / inner + EPSILON)
    pull = inverse * inverse * inverse * joined[:, 64:65] / inner

    def slopes(c, carry):
        spread = spread_of(c)
        a_c = left(pieces(a_ref[...], 3), spread)
        x_wide = x_ref[:, lanes(c)].astype(F32)
        mixed = mixed_ref[:, lanes(c)]
        silu = silu_of(gate_ref[:, lanes(c)].astype(F32))
        gated = mixed * silu
        normed = gated * inverse
        cot = cot_ref[:, lanes(c)].astype(F32)
        gain = gain_ref[:, lanes(c)]
        seq_ref[:, lanes(c)] = (normed * gain).astype(BF16)
        gsum_ref[:, lanes(c)] = jnp.sum(cot * normed, axis=0, keepdims=True)
        slope = (cot * gain * inverse - gated * pull) * silu
        both = pieces(slope, 2)
        ghi_ref[:, lanes(c)] = both[0]
        glo_ref[:, lanes(c)] = both[1]
        skip_c = left(pieces(par_ref[2:3, :] + jnp.zeros((8, heads), F32), 3), spread)[0:1]
        skip_ref[0:1, lanes(c)] = jnp.sum(slope * x_wide, axis=0, keepdims=True)
        q_ref[...] += left(pieces(slope * (mixed - skip_c * x_wide), 3), spread, (1, 1))
        slope_ref[:, lanes(c)] = right(
            c_ref[:, states(c)], pieces(jnp.exp(a_c) * slope, 2), (0, 0)
        )
        return carry

    lax.fori_loop(0, chunks, slopes, 0)

    def peer_copy(o, src, slots, send, recv):
        other = lax.rem(me + o, peers)
        return pltpu.make_async_remote_copy(
            src_ref=src,
            dst_ref=slots.at[o],
            send_sem=send.at[o],
            recv_sem=recv.at[o],
            device_id={"grp": other // n_ctx, "ctx": lax.rem(other, n_ctx)},
            device_id_type=MESH,
        )

    for o in range(1, peers):
        peer_copy(o, gsum_ref, gains_ref, gs_sem, gr_sem).start()

    def backward(c, carry):
        spread, a_c, dt_c = expanded(c)
        last = a_c[tokens - 1 : tokens, :]

        @pl.when(ctx < n_ctx - 1)
        def _():
            backward_copy(c).wait_recv()
            slope_ref[:, lanes(c)] = (
                jnp.exp(last) * later_ref[:, lanes(c)] + slope_ref[:, lanes(c)]
            )

        @pl.when(ctx > 0)
        def _():
            backward_copy(c).start()

        x_wide = x_ref[:, lanes(c)].astype(F32)
        later = later_ref[:, lanes(c)]
        weight = jnp.exp(last - a_c) * dt_c
        ends = weight * right(b_ref[:, states(c)], pieces(later, 2))
        ghi = ghi_ref[:, lanes(c)].astype(F32)
        glo = glo_ref[:, lanes(c)].astype(F32)
        back = ends
        for i in range(per_chunk):
            head = c * per_chunk + i
            hi = jnp.where(lane_head == i, ghi, 0.0).astype(BF16)
            lo = jnp.where(lane_head == i, glo, 0.0).astype(BF16)
            back = back + (
                mm(mhi_ref[head], hi, (0, 0))
                + (mm(mhi_ref[head], lo, (0, 0)) + mm(mlo_ref[head], hi, (0, 0)))
            )
        r_ref[...] += left(pieces(x_wide * back, 3), spread, (1, 1))
        end_ref[0:1, lanes(c)] = jnp.sum(x_wide * ends, axis=0, keepdims=True) + jnp.exp(
            last
        ) * jnp.sum(later * state_ref[:, lanes(c)], axis=0, keepdims=True)
        return carry

    lax.fori_loop(0, chunks, backward, 0)

    def reduced(ref):
        total = jnp.zeros((8, heads), F32)
        for c in range(chunks):
            row = ref[0:1, c * LANES : (c + 1) * LANES] + jnp.zeros((8, LANES), F32)
            total = total + left(pieces(row, 3), spread_of(c), (1, 1))
        return total[0:1]

    skip_slope = reduced(skip_ref)
    end_slope = reduced(end_ref)
    back = r_ref[...]
    token = lax.broadcasted_iota(jnp.int32, (tokens, heads), 0)
    sums = q_ref[...] - back + jnp.where(token == tokens - 1, end_slope, 0.0)
    decay_slope = right(upper, pieces(sums, 3))
    dt = dt_ref[...]
    decay = -rate * dt
    step_slope = back / dt - rate * decay_slope
    hs_ref[...] = jnp.zeros_like(hs_ref)
    hs_ref[0:1, 0:heads] = jnp.sum(decay_slope * decay, axis=0, keepdims=True)
    hs_ref[1:2, 0:heads] = jnp.sum(step_slope * sig_ref[...], axis=0, keepdims=True)
    hs_ref[2:3, 0:heads] = skip_slope
    for o in range(1, peers):
        peer_copy(o, hs_ref, heads_ref, hs_sem, hr_sem).start()
    gain_total = gsum_ref[...]
    for o in range(1, peers):
        peer_copy(o, gsum_ref, gains_ref, gs_sem, gr_sem).wait()
        gain_total = gain_total + gains_ref[o]
    total_ref[...] = gain_total
    head_total = hs_ref[...]
    for o in range(1, peers):
        peer_copy(o, hs_ref, heads_ref, hs_sem, hr_sem).wait()
        head_total = head_total + heads_ref[o]
    head_ref[...] = head_total

    def finish(c, carry):
        @pl.when(ctx < n_ctx - 1)
        def _():
            forward_copy(c).wait_send()

        @pl.when(ctx > 0)
        def _():
            backward_copy(c).wait_send()

        return carry

    lax.fori_loop(0, chunks, finish, 0)


def train(x, gates, b, c, steps, cot, head_params, gain):
    sizes = tuple(lax.axis_size(axis) for axis in ("grp", "ctx", "shd"))
    tokens, inner_local = x.shape
    heads = steps.shape[1]
    chunks = inner_local // LANES
    peers = sizes[0] * sizes[1]
    z = steps + head_params[1]
    dt = jax.nn.softplus(z)
    vmem = pl.BlockSpec(memory_space=pltpu.VMEM)
    dma = pltpu.SemaphoreType.DMA
    scratch = [
        ((tokens, heads), F32),
        ((heads, tokens), F32),
        ((STATE, inner_local), F32),
        ((STATE, inner_local), F32),
        ((STATE, inner_local), F32),
        ((STATE, inner_local), F32),
        ((heads, tokens, tokens), BF16),
        ((heads, tokens, tokens), BF16),
        ((tokens, inner_local), F32),
        ((tokens, inner_local), BF16),
        ((tokens, inner_local), BF16),
        ((tokens, heads), F32),
        ((tokens, heads), F32),
        ((8, inner_local), F32),
        ((8, inner_local), F32),
        ((1, inner_local), F32),
        ((tokens, 128), F32),
        ((max(sizes[2] - 1, 1), tokens, 128), F32),
        ((peers, 1, inner_local), F32),
        ((8, 128), F32),
        ((peers, 8, 128), F32),
    ]
    seq, head_sum, gain_total = pl.pallas_call(
        functools.partial(trained, sizes),
        out_shape=(
            jax.ShapeDtypeStruct((tokens, inner_local), BF16),
            jax.ShapeDtypeStruct((8, 128), F32),
            jax.ShapeDtypeStruct((1, inner_local), F32),
        ),
        in_specs=[vmem] * 11,
        out_specs=(vmem,) * 3,
        scratch_shapes=[pltpu.VMEM(shape, kind) for shape, kind in scratch]
        + [dma((chunks,))] * 4
        + [dma((max(sizes[2] - 1, 1),))] * 2
        + [dma((peers,))] * 4,
        compiler_params=pltpu.CompilerParams(
            collective_id=0, has_side_effects=True, vmem_limit_bytes=63 * 1024 * 1024
        ),
        name="trained",
    )(x, gates, b, c, cot, dt, dt.T, jax.nn.sigmoid(z), head_params, head_params.T, gain[None])
    return seq, head_sum[:3, :heads], gain_total[0]


def on_device(
    train_values,
    train_gates,
    train_writes,
    train_reads,
    train_steps,
    out_cotangent,
    head_params,
    norm_gain,
    slow_heads,
    slow_gain,
    roll_state,
    roll_values,
    roll_gates,
    roll_writes,
    roll_reads,
    roll_steps,
    roll_lengths,
):
    seq_out, head_sum, gain_total = train(
        train_values[0],
        train_gates[0],
        train_writes[0],
        train_reads[0],
        train_steps[0],
        out_cotangent[0],
        head_params,
        norm_gain,
    )
    heads = train_steps.shape[2]
    inner_local = train_values.shape[2]
    inner = inner_local * lax.axis_size("shd")
    blend_gain = KEEP_SHARE * slow_gain + (1.0 - KEEP_SHARE) * (norm_gain - STEP_RATE * gain_total)
    blend_heads = KEEP_SHARE * slow_heads + (1.0 - KEEP_SHARE) * (
        head_params - STEP_RATE * head_sum
    )
    rows = roll_state.shape[0]
    groups = roll_writes.shape[2] // STATE
    active = roll_lengths[:, None] > jnp.arange(STEPS)[None, :]
    steps = jnp.where(active[:, :, None], jax.nn.softplus(roll_steps + blend_heads[1]), 0.0)
    decay = -jnp.exp(blend_heads[0]) * steps
    sums = [decay[:, 0]]
    for k in range(1, STEPS):
        sums.append(sums[-1] + decay[:, k])
    x = roll_values.astype(F32).reshape(rows, STEPS, heads, HEAD_DIM)
    writes = roll_writes.reshape(rows, STEPS, groups, STATE)
    reads = roll_reads.reshape(rows, STEPS, groups, STATE)
    grouped = roll_state.reshape(rows, groups, heads // groups * HEAD_DIM, STATE)
    first = jnp.einsum("rkgn,rgqn->rkgq", reads, grouped, preferred_element_type=F32)
    first = first.reshape(rows, STEPS, heads, HEAD_DIM)
    cross = jnp.einsum("rkgn,rjgn->rkjg", reads, writes, preferred_element_type=F32)
    cross = jnp.repeat(cross, heads // groups, axis=3)
    wide_writes = expand_groups(roll_writes, heads).astype(F32)
    final = jnp.exp(sums[-1])[:, :, None, None] * roll_state.astype(F32)
    for j in range(STEPS):
        share = jnp.exp(sums[-1] - sums[j]) * steps[:, j]
        final = final + (share[:, :, None] * x[:, j])[..., None] * wide_writes[:, j, :, None, :]
    read = []
    for k in range(STEPS):
        now = jnp.exp(sums[k])[:, :, None] * first[:, k] + blend_heads[2][:, None] * x[:, k]
        for j in range(k + 1):
            share = jnp.exp(sums[k] - sums[j]) * steps[:, j] * cross[:, k, j]
            now = now + share[:, :, None] * x[:, j]
        read.append(now)
    gated = jnp.stack(read, axis=1).reshape(rows, STEPS, inner_local)
    gated = gated * jax.nn.silu(roll_gates.astype(F32))
    squares = lax.psum(jnp.sum(gated * gated, axis=2), "shd")
    shown = gated * lax.rsqrt(squares / inner + EPSILON)[..., None] * blend_gain
    roll_out = jnp.where(active[:, :, None], shown, 0.0).astype(BF16)
    return (seq_out[None], head_sum, gain_total, blend_heads, blend_gain, roll_out, final)


def solution(mesh):
    in_specs = (
        P("grp", "ctx", "shd"),
        P("grp", "ctx", "shd"),
        P("grp", "ctx", "shd"),
        P("grp", "ctx", "shd"),
        P("grp", "ctx", "shd"),
        P("grp", "ctx", "shd"),
        P(None, "shd"),
        P("shd"),
        P(None, "shd"),
        P("shd"),
        P(("grp", "ctx"), "shd", None, None),
        P(("grp", "ctx"), None, "shd"),
        P(("grp", "ctx"), None, "shd"),
        P(("grp", "ctx"), None, "shd"),
        P(("grp", "ctx"), None, "shd"),
        P(("grp", "ctx"), None, "shd"),
        P(("grp", "ctx")),
    )
    out_specs = (
        P("grp", "ctx", "shd"),
        P(None, "shd"),
        P("shd"),
        P(None, "shd"),
        P("shd"),
        P(("grp", "ctx"), None, "shd"),
        P(("grp", "ctx"), "shd", None, None),
    )
    return jax.shard_map(
        on_device, mesh=mesh, in_specs=in_specs, out_specs=out_specs, check_vma=False
    )
```

```python
import functools

import jax
import jax.numpy as jnp
from jax import lax
from jax.experimental import pallas as pl
from jax.experimental.pallas import tpu as pltpu
from jax.sharding import PartitionSpec as P

HEAD_DIM = 64
STATE = 128
STEPS = 4
LANES = 256
HOP = 128

HIGHEST = lax.Precision.HIGHEST
MESH = pl.DeviceIdType.MESH
EPSILON = 1e-05
KEEP_SHARE = 0.75
STEP_RATE = 0.001
F32 = jnp.float32
BF16 = jnp.bfloat16


def expand_groups(packed, heads):
    groups = packed.shape[-1] // STATE
    grouped = packed.reshape(packed.shape[:-1] + (groups, STATE))
    return jnp.repeat(grouped, heads // groups, axis=-2)


def pieces(a, count):
    out = []
    for i in range(count):
        piece = a.astype(BF16)
        out.append(piece)
        if i + 1 < count:
            a = a - piece.astype(F32)
    return out


def mm(a, b, dims=(1, 0)):
    return lax.dot_general(
        a, b, (((dims[0],), (dims[1],)), ((), ())), preferred_element_type=F32
    )


def left(parts, b, dims=(1, 0)):
    total = mm(parts[-1], b, dims)
    for part in parts[-2::-1]:
        total = total + mm(part, b, dims)
    return total


def right(a, parts, dims=(1, 0)):
    total = mm(a, parts[-1], dims)
    for part in parts[-2::-1]:
        total = total + mm(a, part, dims)
    return total


def silu_of(gate):
    return gate / (1.0 + jnp.exp(-gate))


def trained(
    sizes,
    x_ref,
    gate_hbm,
    b_ref,
    c_ref,
    cot_hbm,
    dt_ref,
    dtt_ref,
    sig_ref,
    par_ref,
    part_ref,
    gain_ref,
    seq_ref,
    head_ref,
    total_ref,
    a_ref,
    at_ref,
    local_ref,
    state_ref,
    slope_ref,
    later_ref,
    mhi_ref,
    mlo_ref,
    mixed_ref,
    gate_ref,
    cot_ref,
    q_ref,
    r_ref,
    skip_ref,
    end_ref,
    gsum_ref,
    ex_ref,
    exr_ref,
    gains_ref,
    hs_ref,
    heads_ref,
    fs_sem,
    fr_sem,
    bs_sem,
    br_sem,
    es_sem,
    er_sem,
    gs_sem,
    gr_sem,
    hs_sem,
    hr_sem,
    in_sem,
):
    n_grp, n_ctx, n_shd = sizes
    tokens, inner_local = x_ref.shape
    heads = dt_ref.shape[1]
    groups = b_ref.shape[1] // STATE
    chunks = inner_local // LANES
    per_group = chunks // groups
    per_chunk = LANES // HEAD_DIM
    inner = inner_local * n_shd
    grp = lax.axis_index("grp")
    ctx = lax.axis_index("ctx")
    shd = lax.axis_index("shd")
    peers = n_grp * n_ctx
    me = grp * n_ctx + ctx

    gate_load = pltpu.make_async_copy(gate_hbm, gate_ref, in_sem.at[0])
    cot_load = pltpu.make_async_copy(cot_hbm, cot_ref, in_sem.at[1])
    gate_load.start()
    cot_load.start()
    barrier = pltpu.get_barrier_semaphore()
    for o in range(1, peers):
        other = lax.rem(me + o, peers)
        pl.semaphore_signal(
            barrier,
            inc=1,
            device_id={"grp": other // n_ctx, "ctx": lax.rem(other, n_ctx)},
            device_id_type=MESH,
        )
    for o in range(1, n_shd):
        pl.semaphore_signal(
            barrier, inc=1, device_id={"shd": lax.rem(shd + o, n_shd)}, device_id_type=MESH
        )

    row_t = lax.broadcasted_iota(jnp.int32, (tokens, tokens), 0)
    col_t = lax.broadcasted_iota(jnp.int32, (tokens, tokens), 1)
    causal = row_t >= col_t
    lower = jnp.where(causal, 1.0, 0.0).astype(BF16)
    upper = jnp.where(row_t <= col_t, 1.0, 0.0).astype(BF16)
    lane_head = lax.broadcasted_iota(jnp.int32, (tokens, LANES), 1) // HEAD_DIM
    head_row = lax.broadcasted_iota(jnp.int32, (heads, LANES), 0)
    head_lane = lax.broadcasted_iota(jnp.int32, (heads, LANES), 1) // HEAD_DIM

    rate = jnp.exp(par_ref[0:1, :])
    decay = -rate * dt_ref[...]
    a_ref[...] = right(lower, pieces(decay, 3))
    decay_t = -jnp.exp(part_ref[:, 0:1]) * dtt_ref[...]
    at_ref[...] = left(pieces(decay_t, 3), upper)

    def spread_of(c):
        return jnp.where(head_row == c * per_chunk + head_lane, 1.0, 0.0).astype(BF16)

    def lanes(c):
        return pl.ds(pl.multiple_of(c * LANES, LANES), LANES)

    def states(c):
        return pl.ds(pl.multiple_of(c // per_group * STATE, STATE), STATE)

    def expanded(c):
        spread = spread_of(c)
        a_c = left(pieces(a_ref[...], 3), spread)
        dt_c = left(pieces(dt_ref[...], 3), spread)
        return spread, a_c, dt_c

    @pl.when(ctx == 0)
    def _():
        state_ref[...] = jnp.zeros_like(state_ref)

    @pl.when(ctx == n_ctx - 1)
    def _():
        later_ref[...] = jnp.zeros_like(later_ref)

    pl.semaphore_wait(barrier, peers - 1 + n_shd - 1)

    def forward_copy(j):
        place = pl.ds(pl.multiple_of(j * HOP, HOP), HOP)
        return pltpu.make_async_remote_copy(
            src_ref=local_ref.at[:, place],
            dst_ref=state_ref.at[:, place],
            send_sem=fs_sem.at[j],
            recv_sem=fr_sem.at[j],
            device_id={"ctx": lax.rem(ctx + 1, n_ctx)},
            device_id_type=MESH,
        )

    def backward_copy(j):
        place = pl.ds(pl.multiple_of(j * HOP, HOP), HOP)
        return pltpu.make_async_remote_copy(
            src_ref=slope_ref.at[:, place],
            dst_ref=later_ref.at[:, place],
            send_sem=bs_sem.at[j],
            recv_sem=br_sem.at[j],
            device_id={"ctx": lax.rem(ctx + n_ctx - 1, n_ctx)},
            device_id_type=MESH,
        )

    ex_ref[...] = jnp.zeros_like(ex_ref)
    q_ref[...] = jnp.zeros_like(q_ref)
    r_ref[...] = jnp.zeros_like(r_ref)

    def relay(c, has_source, has_target, copy, mine_ref, came_ref, factor):
        for half in range(LANES // HOP):
            j = c * (LANES // HOP) + half
            place = pl.ds(pl.multiple_of(j * HOP, HOP), HOP)

            @pl.when(has_source)
            def _():
                copy(j).wait_recv()
                mine_ref[:, place] = (
                    factor[:, half * HOP : (half + 1) * HOP] * came_ref[:, place]
                    + mine_ref[:, place]
                )

            @pl.when(has_target)
            def _():
                copy(j).start()

    def fold(a):
        total = a[:, :128]
        for i in range(128, a.shape[1], 128):
            total = total + a[:, i : i + 128]
        return total

    def forward(c, carry):
        squares, products = carry
        spread, a_c, dt_c = expanded(c)
        last = a_c[tokens - 1 : tokens, :]
        x_wide = x_ref[:, lanes(c)].astype(F32)
        fresh = jnp.exp(last - a_c) * dt_c * x_wide
        local_ref[:, lanes(c)] = right(b_ref[:, states(c)], pieces(fresh, 2), (0, 0))
        scores = mm(c_ref[:, states(c)], b_ref[:, states(c)], (1, 1))
        skip_c = left(pieces(par_ref[2:3, :] + jnp.zeros((8, heads), F32), 3), spread)[0:1]
        mixed = skip_c * x_wide
        for i in range(per_chunk):
            head = c * per_chunk + i
            gap = a_c[:, i * HEAD_DIM : i * HEAD_DIM + 1] - at_ref[pl.ds(head, 1), :]
            weight = jnp.exp(jnp.where(causal, gap, -1e30)) * dtt_ref[pl.ds(head, 1), :]
            both = pieces(scores * weight, 2)
            mhi_ref[head] = both[0]
            mlo_ref[head] = both[1]
            own = jnp.where(lane_head == i, x_wide, 0.0).astype(BF16)
            mixed = mixed + left(both, own)
        mixed_ref[:, lanes(c)] = mixed
        relay(c, ctx > 0, ctx < n_ctx - 1, forward_copy, local_ref, state_ref, jnp.exp(last))
        read_in = right(c_ref[:, states(c)], pieces(state_ref[:, lanes(c)], 2))
        mixed = mixed_ref[:, lanes(c)] + jnp.exp(a_c) * read_in

        @pl.when(c == 0)
        def _():
            gate_load.wait()
            cot_load.wait()

        mixed_ref[:, lanes(c)] = mixed
        gated = mixed * silu_of(gate_ref[:, lanes(c)].astype(F32))
        weighted = cot_ref[:, lanes(c)].astype(F32) * gain_ref[:, lanes(c)]
        return (squares + fold(gated * gated), products + fold(weighted * gated))

    zero = jnp.zeros((tokens, 128), F32)
    squares, products = lax.fori_loop(0, chunks, forward, (zero, zero))
    lane = lax.broadcasted_iota(jnp.int32, (tokens, 128), 1)
    ex_ref[...] = jnp.where(
        lane < 64,
        jnp.sum(squares, axis=1, keepdims=True),
        jnp.sum(products, axis=1, keepdims=True),
    )
    copies = []
    for o in range(1, n_shd):
        copies.append(
            pltpu.make_async_remote_copy(
                src_ref=ex_ref,
                dst_ref=exr_ref.at[o - 1],
                send_sem=es_sem.at[o - 1],
                recv_sem=er_sem.at[o - 1],
                device_id={"shd": lax.rem(shd + o, n_shd)},
                device_id_type=MESH,
            )
        )
        copies[-1].start()
    joined = ex_ref[...]
    for o in range(1, n_shd):
        copies[o - 1].wait()
        joined = joined + exr_ref[o - 1]
    inverse = lax.rsqrt(joined[:, 0:1] / inner + EPSILON)
    pull = inverse * inverse * inverse * joined[:, 64:65] / inner

    def peer_copy(o, src, slots, send, recv):
        other = lax.rem(me + o, peers)
        return pltpu.make_async_remote_copy(
            src_ref=src,
            dst_ref=slots.at[o],
            send_sem=send.at[o],
            recv_sem=recv.at[o],
            device_id={"grp": other // n_ctx, "ctx": lax.rem(other, n_ctx)},
            device_id_type=MESH,
        )

    def backward(c, carry):
        spread, a_c, dt_c = expanded(c)
        last = a_c[tokens - 1 : tokens, :]
        x_wide = x_ref[:, lanes(c)].astype(F32)
        mixed = mixed_ref[:, lanes(c)]
        silu = silu_of(gate_ref[:, lanes(c)].astype(F32))
        gated = mixed * silu
        normed = gated * inverse
        cot = cot_ref[:, lanes(c)].astype(F32)
        gain = gain_ref[:, lanes(c)]
        seq_ref[:, lanes(c)] = (normed * gain).astype(BF16)
        gsum_ref[:, lanes(c)] = jnp.sum(cot * normed, axis=0, keepdims=True)
        slope = (cot * gain * inverse - gated * pull) * silu
        slope_ref[:, lanes(c)] = right(
            c_ref[:, states(c)], pieces(jnp.exp(a_c) * slope, 2), (0, 0)
        )
        skip_c = left(pieces(par_ref[2:3, :] + jnp.zeros((8, heads), F32), 3), spread)[0:1]
        skip_ref[0:1, lanes(c)] = jnp.sum(slope * x_wide, axis=0, keepdims=True)
        q_ref[...] += left(pieces(slope * (mixed - skip_c * x_wide), 3), spread, (1, 1))
        ghi, glo = (piece.astype(F32) for piece in pieces(slope, 2))
        back = jnp.zeros((tokens, LANES), F32)
        for i in range(per_chunk):
            head = c * per_chunk + i
            hi = jnp.where(lane_head == i, ghi, 0.0).astype(BF16)
            lo = jnp.where(lane_head == i, glo, 0.0).astype(BF16)
            back = back + (
                mm(mhi_ref[head], hi, (0, 0))
                + (mm(mhi_ref[head], lo, (0, 0)) + mm(mlo_ref[head], hi, (0, 0)))
            )
        mixed_ref[:, lanes(c)] = back

        @pl.when(c == chunks - 1)
        def _():
            for o in range(1, peers):
                peer_copy(o, gsum_ref, gains_ref, gs_sem, gr_sem).start()

        relay(c, ctx < n_ctx - 1, ctx > 0, backward_copy, slope_ref, later_ref, jnp.exp(last))
        later = later_ref[:, lanes(c)]
        ends = jnp.exp(last - a_c) * dt_c * right(b_ref[:, states(c)], pieces(later, 2))
        back = mixed_ref[:, lanes(c)] + ends
        r_ref[...] += left(pieces(x_wide * back, 3), spread, (1, 1))
        end_ref[0:1, lanes(c)] = jnp.sum(x_wide * ends, axis=0, keepdims=True) + jnp.exp(
            last
        ) * jnp.sum(later * state_ref[:, lanes(c)], axis=0, keepdims=True)
        return carry

    lax.fori_loop(0, chunks, backward, 0)

    def reduced(ref):
        total = jnp.zeros((8, heads), F32)
        for c in range(chunks):
            row = ref[0:1, c * LANES : (c + 1) * LANES] + jnp.zeros((8, LANES), F32)
            total = total + left(pieces(row, 3), spread_of(c), (1, 1))
        return total[0:1]

    skip_slope = reduced(skip_ref)
    end_slope = reduced(end_ref)
    back = r_ref[...]
    token = lax.broadcasted_iota(jnp.int32, (tokens, heads), 0)
    sums = q_ref[...] - back + jnp.where(token == tokens - 1, end_slope, 0.0)
    decay_slope = right(upper, pieces(sums, 3))
    dt = dt_ref[...]
    decay = -rate * dt
    step_slope = back / dt - rate * decay_slope
    hs_ref[...] = jnp.zeros_like(hs_ref)
    hs_ref[0:1, 0:heads] = jnp.sum(decay_slope * decay, axis=0, keepdims=True)
    hs_ref[1:2, 0:heads] = jnp.sum(step_slope * sig_ref[...], axis=0, keepdims=True)
    hs_ref[2:3, 0:heads] = skip_slope
    for o in range(1, peers):
        peer_copy(o, hs_ref, heads_ref, hs_sem, hr_sem).start()
    gain_total = gsum_ref[...]
    for o in range(1, peers):
        peer_copy(o, gsum_ref, gains_ref, gs_sem, gr_sem).wait()
        gain_total = gain_total + gains_ref[o]
    total_ref[...] = gain_total
    head_total = hs_ref[...]
    for o in range(1, peers):
        peer_copy(o, hs_ref, heads_ref, hs_sem, hr_sem).wait()
        head_total = head_total + heads_ref[o]
    head_ref[...] = head_total

    def finish(c, carry):
        @pl.when(ctx < n_ctx - 1)
        def _():
            forward_copy(c).wait_send()

        @pl.when(ctx > 0)
        def _():
            backward_copy(c).wait_send()

        return carry

    lax.fori_loop(0, chunks * (LANES // HOP), finish, 0)


def train(x, gates, b, c, steps, cot, head_params, gain):
    sizes = tuple(lax.axis_size(axis) for axis in ("grp", "ctx", "shd"))
    tokens, inner_local = x.shape
    heads = steps.shape[1]
    chunks = inner_local // LANES
    peers = sizes[0] * sizes[1]
    z = steps + head_params[1]
    dt = jax.nn.softplus(z)
    vmem = pl.BlockSpec(memory_space=pltpu.VMEM)
    whole = pl.BlockSpec(memory_space=pl.ANY)
    dma = pltpu.SemaphoreType.DMA
    scratch = [
        ((tokens, heads), F32),
        ((heads, tokens), F32),
        ((STATE, inner_local), F32),
        ((STATE, inner_local), F32),
        ((STATE, inner_local), F32),
        ((STATE, inner_local), F32),
        ((heads, tokens, tokens), BF16),
        ((heads, tokens, tokens), BF16),
        ((tokens, inner_local), F32),
        ((tokens, inner_local), BF16),
        ((tokens, inner_local), BF16),
        ((tokens, heads), F32),
        ((tokens, heads), F32),
        ((8, inner_local), F32),
        ((8, inner_local), F32),
        ((1, inner_local), F32),
        ((tokens, 128), F32),
        ((max(sizes[2] - 1, 1), tokens, 128), F32),
        ((peers, 1, inner_local), F32),
        ((8, 128), F32),
        ((peers, 8, 128), F32),
    ]
    seq, head_sum, gain_total = pl.pallas_call(
        functools.partial(trained, sizes),
        out_shape=(
            jax.ShapeDtypeStruct((tokens, inner_local), BF16),
            jax.ShapeDtypeStruct((8, 128), F32),
            jax.ShapeDtypeStruct((1, inner_local), F32),
        ),
        in_specs=[vmem, whole, vmem, vmem, whole] + [vmem] * 6,
        out_specs=(vmem,) * 3,
        scratch_shapes=[pltpu.VMEM(shape, kind) for shape, kind in scratch]
        + [dma((chunks * (LANES // HOP),))] * 4
        + [dma((max(sizes[2] - 1, 1),))] * 2
        + [dma((peers,))] * 4
        + [dma((2,))],
        compiler_params=pltpu.CompilerParams(
            collective_id=0, has_side_effects=True, vmem_limit_bytes=63 * 1024 * 1024
        ),
        name="trained",
    )(x, gates, b, c, cot, dt, dt.T, jax.nn.sigmoid(z), head_params, head_params.T, gain[None])
    return seq, head_sum[:3, :heads], gain_total[0]


def on_device(
    train_values,
    train_gates,
    train_writes,
    train_reads,
    train_steps,
    out_cotangent,
    head_params,
    norm_gain,
    slow_heads,
    slow_gain,
    roll_state,
    roll_values,
    roll_gates,
    roll_writes,
    roll_reads,
    roll_steps,
    roll_lengths,
):
    seq_out, head_sum, gain_total = train(
        train_values[0],
        train_gates[0],
        train_writes[0],
        train_reads[0],
        train_steps[0],
        out_cotangent[0],
        head_params,
        norm_gain,
    )
    heads = train_steps.shape[2]
    inner_local = train_values.shape[2]
    inner = inner_local * lax.axis_size("shd")
    blend_gain = KEEP_SHARE * slow_gain + (1.0 - KEEP_SHARE) * (norm_gain - STEP_RATE * gain_total)
    blend_heads = KEEP_SHARE * slow_heads + (1.0 - KEEP_SHARE) * (
        head_params - STEP_RATE * head_sum
    )
    rows = roll_state.shape[0]
    groups = roll_writes.shape[2] // STATE
    active = roll_lengths[:, None] > jnp.arange(STEPS)[None, :]
    steps = jnp.where(active[:, :, None], jax.nn.softplus(roll_steps + blend_heads[1]), 0.0)
    decay = -jnp.exp(blend_heads[0]) * steps
    sums = [decay[:, 0]]
    for k in range(1, STEPS):
        sums.append(sums[-1] + decay[:, k])
    x = roll_values.astype(F32).reshape(rows, STEPS, heads, HEAD_DIM)
    writes = roll_writes.reshape(rows, STEPS, groups, STATE)
    reads = roll_reads.reshape(rows, STEPS, groups, STATE)
    grouped = roll_state.reshape(rows, groups, heads // groups * HEAD_DIM, STATE)
    first = jnp.einsum("rkgn,rgqn->rkgq", reads, grouped, preferred_element_type=F32)
    first = first.reshape(rows, STEPS, heads, HEAD_DIM)
    cross = jnp.einsum("rkgn,rjgn->rkjg", reads, writes, preferred_element_type=F32)
    cross = jnp.repeat(cross, heads // groups, axis=3)
    wide_writes = expand_groups(roll_writes, heads).astype(F32)
    final = jnp.exp(sums[-1])[:, :, None, None] * roll_state.astype(F32)
    for j in range(STEPS):
        share = jnp.exp(sums[-1] - sums[j]) * steps[:, j]
        final = final + (share[:, :, None] * x[:, j])[..., None] * wide_writes[:, j, :, None, :]
    read = []
    for k in range(STEPS):
        now = jnp.exp(sums[k])[:, :, None] * first[:, k] + blend_heads[2][:, None] * x[:, k]
        for j in range(k + 1):
            share = jnp.exp(sums[k] - sums[j]) * steps[:, j] * cross[:, k, j]
            now = now + share[:, :, None] * x[:, j]
        read.append(now)
    gated = jnp.stack(read, axis=1).reshape(rows, STEPS, inner_local)
    gated = gated * jax.nn.silu(roll_gates.astype(F32))
    squares = lax.psum(jnp.sum(gated * gated, axis=2), "shd")
    shown = gated * lax.rsqrt(squares / inner + EPSILON)[..., None] * blend_gain
    roll_out = jnp.where(active[:, :, None], shown, 0.0).astype(BF16)
    return (seq_out[None], head_sum, gain_total, blend_heads, blend_gain, roll_out, final)


def solution(mesh):
    in_specs = (
        P("grp", "ctx", "shd"),
        P("grp", "ctx", "shd"),
        P("grp", "ctx", "shd"),
        P("grp", "ctx", "shd"),
        P("grp", "ctx", "shd"),
        P("grp", "ctx", "shd"),
        P(None, "shd"),
        P("shd"),
        P(None, "shd"),
        P("shd"),
        P(("grp", "ctx"), "shd", None, None),
        P(("grp", "ctx"), None, "shd"),
        P(("grp", "ctx"), None, "shd"),
        P(("grp", "ctx"), None, "shd"),
        P(("grp", "ctx"), None, "shd"),
        P(("grp", "ctx"), None, "shd"),
        P(("grp", "ctx")),
    )
    out_specs = (
        P("grp", "ctx", "shd"),
        P(None, "shd"),
        P("shd"),
        P(None, "shd"),
        P("shd"),
        P(("grp", "ctx"), None, "shd"),
        P(("grp", "ctx"), "shd", None, None),
    )
    return jax.shard_map(
        on_device, mesh=mesh, in_specs=in_specs, out_specs=out_specs, check_vma=False
    )
```

```python
import functools

import jax
import jax.numpy as jnp
from jax import lax
from jax.experimental import pallas as pl
from jax.experimental.pallas import tpu as pltpu
from jax.sharding import PartitionSpec as P

HEAD_DIM = 64
STATE = 128
STEPS = 4
LANES = 256
HOP = 128
HOP_ROWS = 64
SLABS = STATE // HOP_ROWS
HOPS = LANES // HOP * SLABS

HIGHEST = lax.Precision.HIGHEST
MESH = pl.DeviceIdType.MESH
EPSILON = 1e-05
KEEP_SHARE = 0.75
STEP_RATE = 0.001
F32 = jnp.float32
BF16 = jnp.bfloat16


def expand_groups(packed, heads):
    groups = packed.shape[-1] // STATE
    grouped = packed.reshape(packed.shape[:-1] + (groups, STATE))
    return jnp.repeat(grouped, heads // groups, axis=-2)


def pieces(a, count):
    out = []
    for i in range(count):
        piece = a.astype(BF16)
        out.append(piece)
        if i + 1 < count:
            a = a - piece.astype(F32)
    return out


def mm(a, b, dims=(1, 0)):
    return lax.dot_general(
        a, b, (((dims[0],), (dims[1],)), ((), ())), preferred_element_type=F32
    )


def left(parts, b, dims=(1, 0)):
    total = mm(parts[-1], b, dims)
    for part in parts[-2::-1]:
        total = total + mm(part, b, dims)
    return total


def right(a, parts, dims=(1, 0)):
    total = mm(a, parts[-1], dims)
    for part in parts[-2::-1]:
        total = total + mm(a, part, dims)
    return total


def silu_of(gate):
    return gate / (1.0 + jnp.exp(-gate))


def trained(
    sizes,
    x_ref,
    gate_hbm,
    b_ref,
    c_ref,
    cot_hbm,
    dt_ref,
    dtt_ref,
    sig_ref,
    par_ref,
    part_ref,
    gain_ref,
    seq_ref,
    head_ref,
    total_ref,
    a_ref,
    at_ref,
    local_ref,
    state_ref,
    slope_ref,
    later_ref,
    mhi_ref,
    mlo_ref,
    mixed_ref,
    gate_ref,
    cot_ref,
    q_ref,
    r_ref,
    skip_ref,
    end_ref,
    gsum_ref,
    ex_ref,
    exr_ref,
    gains_ref,
    hs_ref,
    heads_ref,
    fs_sem,
    fr_sem,
    bs_sem,
    br_sem,
    es_sem,
    er_sem,
    gs_sem,
    gr_sem,
    hs_sem,
    hr_sem,
    in_sem,
):
    n_grp, n_ctx, n_shd = sizes
    tokens, inner_local = x_ref.shape
    heads = dt_ref.shape[1]
    groups = b_ref.shape[1] // STATE
    chunks = inner_local // LANES
    per_group = chunks // groups
    per_chunk = LANES // HEAD_DIM
    inner = inner_local * n_shd
    grp = lax.axis_index("grp")
    ctx = lax.axis_index("ctx")
    shd = lax.axis_index("shd")
    peers = n_grp * n_ctx
    me = grp * n_ctx + ctx

    gate_load = pltpu.make_async_copy(gate_hbm, gate_ref, in_sem.at[0])
    cot_load = pltpu.make_async_copy(cot_hbm, cot_ref, in_sem.at[1])
    gate_load.start()
    cot_load.start()
    barrier = pltpu.get_barrier_semaphore()
    for o in range(1, peers):
        other = lax.rem(me + o, peers)
        pl.semaphore_signal(
            barrier,
            inc=1,
            device_id={"grp": other // n_ctx, "ctx": lax.rem(other, n_ctx)},
            device_id_type=MESH,
        )
    for o in range(1, n_shd):
        pl.semaphore_signal(
            barrier, inc=1, device_id={"shd": lax.rem(shd + o, n_shd)}, device_id_type=MESH
        )

    row_t = lax.broadcasted_iota(jnp.int32, (tokens, tokens), 0)
    col_t = lax.broadcasted_iota(jnp.int32, (tokens, tokens), 1)
    causal = row_t >= col_t
    lower = jnp.where(causal, 1.0, 0.0).astype(BF16)
    upper = jnp.where(row_t <= col_t, 1.0, 0.0).astype(BF16)
    lane_head = lax.broadcasted_iota(jnp.int32, (tokens, LANES), 1) // HEAD_DIM
    head_row = lax.broadcasted_iota(jnp.int32, (heads, LANES), 0)
    head_lane = lax.broadcasted_iota(jnp.int32, (heads, LANES), 1) // HEAD_DIM

    rate = jnp.exp(par_ref[0:1, :])
    decay = -rate * dt_ref[...]
    a_ref[...] = right(lower, pieces(decay, 3))
    decay_t = -jnp.exp(part_ref[:, 0:1]) * dtt_ref[...]
    at_ref[...] = left(pieces(decay_t, 3), upper)

    def spread_of(c):
        return jnp.where(head_row == c * per_chunk + head_lane, 1.0, 0.0).astype(BF16)

    def lanes(c):
        return pl.ds(pl.multiple_of(c * LANES, LANES), LANES)

    def states(c):
        return pl.ds(pl.multiple_of(c // per_group * STATE, STATE), STATE)

    def expanded(c):
        spread = spread_of(c)
        a_c = left(pieces(a_ref[...], 3), spread)
        dt_c = left(pieces(dt_ref[...], 3), spread)
        return spread, a_c, dt_c

    @pl.when(ctx == 0)
    def _():
        state_ref[...] = jnp.zeros_like(state_ref)

    @pl.when(ctx == n_ctx - 1)
    def _():
        later_ref[...] = jnp.zeros_like(later_ref)

    pl.semaphore_wait(barrier, peers - 1 + n_shd - 1)

    def hop(j):
        return (
            pl.ds(pl.multiple_of(j % SLABS * HOP_ROWS, HOP_ROWS), HOP_ROWS),
            pl.ds(pl.multiple_of(j // SLABS * HOP, HOP), HOP),
        )

    def forward_copy(j):
        place = hop(j)
        return pltpu.make_async_remote_copy(
            src_ref=local_ref.at[place],
            dst_ref=state_ref.at[place],
            send_sem=fs_sem.at[j],
            recv_sem=fr_sem.at[j],
            device_id={"ctx": lax.rem(ctx + 1, n_ctx)},
            device_id_type=MESH,
        )

    def backward_copy(j):
        place = hop(j)
        return pltpu.make_async_remote_copy(
            src_ref=slope_ref.at[place],
            dst_ref=later_ref.at[place],
            send_sem=bs_sem.at[j],
            recv_sem=br_sem.at[j],
            device_id={"ctx": lax.rem(ctx + n_ctx - 1, n_ctx)},
            device_id_type=MESH,
        )

    ex_ref[...] = jnp.zeros_like(ex_ref)
    q_ref[...] = jnp.zeros_like(q_ref)
    r_ref[...] = jnp.zeros_like(r_ref)

    def relay(c, has_source, has_target, copy, mine_ref, came_ref, factor):
        for part in range(HOPS):
            j = c * HOPS + part
            place = hop(j)
            lane = part // SLABS * HOP

            @pl.when(has_source)
            def _():
                copy(j).wait_recv()
                mine_ref[place] = (
                    factor[:, lane : lane + HOP] * came_ref[place] + mine_ref[place]
                )

                @pl.when(has_target)
                def _():
                    copy(j).start()

    def lead(c, is_first, copy):
        @pl.when(is_first)
        def _():
            for part in range(HOPS):
                copy(c * HOPS + part).start()

    def fold(a):
        total = a[:, :128]
        for i in range(128, a.shape[1], 128):
            total = total + a[:, i : i + 128]
        return total

    def forward(c, carry):
        squares, products = carry
        spread, a_c, dt_c = expanded(c)
        last = a_c[tokens - 1 : tokens, :]
        x_wide = x_ref[:, lanes(c)].astype(F32)
        fresh = jnp.exp(last - a_c) * dt_c * x_wide
        local_ref[:, lanes(c)] = right(b_ref[:, states(c)], pieces(fresh, 2), (0, 0))
        lead(c, ctx == 0, forward_copy)
        scores = mm(c_ref[:, states(c)], b_ref[:, states(c)], (1, 1))
        skip_c = left(pieces(par_ref[2:3, :] + jnp.zeros((8, heads), F32), 3), spread)[0:1]
        mixed = skip_c * x_wide
        for i in range(per_chunk):
            head = c * per_chunk + i
            gap = a_c[:, i * HEAD_DIM : i * HEAD_DIM + 1] - at_ref[pl.ds(head, 1), :]
            weight = jnp.exp(jnp.where(causal, gap, -1e30)) * dtt_ref[pl.ds(head, 1), :]
            both = pieces(scores * weight, 2)
            mhi_ref[head] = both[0]
            mlo_ref[head] = both[1]
            own = jnp.where(lane_head == i, x_wide, 0.0).astype(BF16)
            mixed = mixed + left(both, own)
        mixed_ref[:, lanes(c)] = mixed
        relay(c, ctx > 0, ctx < n_ctx - 1, forward_copy, local_ref, state_ref, jnp.exp(last))
        read_in = right(c_ref[:, states(c)], pieces(state_ref[:, lanes(c)], 2))
        mixed = mixed_ref[:, lanes(c)] + jnp.exp(a_c) * read_in

        @pl.when(c == 0)
        def _():
            gate_load.wait()
            cot_load.wait()

        mixed_ref[:, lanes(c)] = mixed
        gated = mixed * silu_of(gate_ref[:, lanes(c)].astype(F32))
        weighted = cot_ref[:, lanes(c)].astype(F32) * gain_ref[:, lanes(c)]
        return (squares + fold(gated * gated), products + fold(weighted * gated))

    zero = jnp.zeros((tokens, 128), F32)
    squares, products = lax.fori_loop(0, chunks, forward, (zero, zero))
    lane = lax.broadcasted_iota(jnp.int32, (tokens, 128), 1)
    ex_ref[...] = jnp.where(
        lane < 64,
        jnp.sum(squares, axis=1, keepdims=True),
        jnp.sum(products, axis=1, keepdims=True),
    )
    copies = []
    for o in range(1, n_shd):
        copies.append(
            pltpu.make_async_remote_copy(
                src_ref=ex_ref,
                dst_ref=exr_ref.at[o - 1],
                send_sem=es_sem.at[o - 1],
                recv_sem=er_sem.at[o - 1],
                device_id={"shd": lax.rem(shd + o, n_shd)},
                device_id_type=MESH,
            )
        )
        copies[-1].start()
    joined = ex_ref[...]
    for o in range(1, n_shd):
        copies[o - 1].wait()
        joined = joined + exr_ref[o - 1]
    inverse = lax.rsqrt(joined[:, 0:1] / inner + EPSILON)
    pull = inverse * inverse * inverse * joined[:, 64:65] / inner

    def peer_copy(o, src, slots, send, recv):
        other = lax.rem(me + o, peers)
        return pltpu.make_async_remote_copy(
            src_ref=src,
            dst_ref=slots.at[o],
            send_sem=send.at[o],
            recv_sem=recv.at[o],
            device_id={"grp": other // n_ctx, "ctx": lax.rem(other, n_ctx)},
            device_id_type=MESH,
        )

    def backward(c, carry):
        spread, a_c, dt_c = expanded(c)
        last = a_c[tokens - 1 : tokens, :]
        x_wide = x_ref[:, lanes(c)].astype(F32)
        mixed = mixed_ref[:, lanes(c)]
        silu = silu_of(gate_ref[:, lanes(c)].astype(F32))
        gated = mixed * silu
        normed = gated * inverse
        cot = cot_ref[:, lanes(c)].astype(F32)
        gain = gain_ref[:, lanes(c)]
        seq_ref[:, lanes(c)] = (normed * gain).astype(BF16)
        gsum_ref[:, lanes(c)] = jnp.sum(cot * normed, axis=0, keepdims=True)
        slope = (cot * gain * inverse - gated * pull) * silu
        slope_ref[:, lanes(c)] = right(
            c_ref[:, states(c)], pieces(jnp.exp(a_c) * slope, 2), (0, 0)
        )
        lead(c, ctx == n_ctx - 1, backward_copy)
        skip_c = left(pieces(par_ref[2:3, :] + jnp.zeros((8, heads), F32), 3), spread)[0:1]
        skip_ref[0:1, lanes(c)] = jnp.sum(slope * x_wide, axis=0, keepdims=True)
        q_ref[...] += left(pieces(slope * (mixed - skip_c * x_wide), 3), spread, (1, 1))
        ghi, glo = (piece.astype(F32) for piece in pieces(slope, 2))
        back = jnp.zeros((tokens, LANES), F32)
        for i in range(per_chunk):
            head = c * per_chunk + i
            hi = jnp.where(lane_head == i, ghi, 0.0).astype(BF16)
            lo = jnp.where(lane_head == i, glo, 0.0).astype(BF16)
            back = back + (
                mm(mhi_ref[head], hi, (0, 0))
                + (mm(mhi_ref[head], lo, (0, 0)) + mm(mlo_ref[head], hi, (0, 0)))
            )
        mixed_ref[:, lanes(c)] = back

        @pl.when(c == chunks - 1)
        def _():
            for o in range(1, peers):
                peer_copy(o, gsum_ref, gains_ref, gs_sem, gr_sem).start()

        relay(c, ctx < n_ctx - 1, ctx > 0, backward_copy, slope_ref, later_ref, jnp.exp(last))
        later = later_ref[:, lanes(c)]
        ends = jnp.exp(last - a_c) * dt_c * right(b_ref[:, states(c)], pieces(later, 2))
        back = mixed_ref[:, lanes(c)] + ends
        r_ref[...] += left(pieces(x_wide * back, 3), spread, (1, 1))
        end_ref[0:1, lanes(c)] = jnp.sum(x_wide * ends, axis=0, keepdims=True) + jnp.exp(
            last
        ) * jnp.sum(later * state_ref[:, lanes(c)], axis=0, keepdims=True)
        return carry

    lax.fori_loop(0, chunks, backward, 0)

    def reduced(ref):
        total = jnp.zeros((8, heads), F32)
        for c in range(chunks):
            row = ref[0:1, c * LANES : (c + 1) * LANES] + jnp.zeros((8, LANES), F32)
            total = total + left(pieces(row, 3), spread_of(c), (1, 1))
        return total[0:1]

    skip_slope = reduced(skip_ref)
    end_slope = reduced(end_ref)
    back = r_ref[...]
    token = lax.broadcasted_iota(jnp.int32, (tokens, heads), 0)
    sums = q_ref[...] - back + jnp.where(token == tokens - 1, end_slope, 0.0)
    decay_slope = right(upper, pieces(sums, 3))
    dt = dt_ref[...]
    decay = -rate * dt
    step_slope = back / dt - rate * decay_slope
    hs_ref[...] = jnp.zeros_like(hs_ref)
    hs_ref[0:1, 0:heads] = jnp.sum(decay_slope * decay, axis=0, keepdims=True)
    hs_ref[1:2, 0:heads] = jnp.sum(step_slope * sig_ref[...], axis=0, keepdims=True)
    hs_ref[2:3, 0:heads] = skip_slope
    for o in range(1, peers):
        peer_copy(o, hs_ref, heads_ref, hs_sem, hr_sem).start()
    gain_total = gsum_ref[...]
    for o in range(1, peers):
        peer_copy(o, gsum_ref, gains_ref, gs_sem, gr_sem).wait()
        gain_total = gain_total + gains_ref[o]
    total_ref[...] = gain_total
    head_total = hs_ref[...]
    for o in range(1, peers):
        peer_copy(o, hs_ref, heads_ref, hs_sem, hr_sem).wait()
        head_total = head_total + heads_ref[o]
    head_ref[...] = head_total

    def finish(c, carry):
        @pl.when(ctx < n_ctx - 1)
        def _():
            forward_copy(c).wait_send()

        @pl.when(ctx > 0)
        def _():
            backward_copy(c).wait_send()

        return carry

    lax.fori_loop(0, chunks * HOPS, finish, 0)


def train(x, gates, b, c, steps, cot, head_params, gain):
    sizes = tuple(lax.axis_size(axis) for axis in ("grp", "ctx", "shd"))
    tokens, inner_local = x.shape
    heads = steps.shape[1]
    chunks = inner_local // LANES
    peers = sizes[0] * sizes[1]
    z = steps + head_params[1]
    dt = jax.nn.softplus(z)
    vmem = pl.BlockSpec(memory_space=pltpu.VMEM)
    whole = pl.BlockSpec(memory_space=pl.ANY)
    dma = pltpu.SemaphoreType.DMA
    scratch = [
        ((tokens, heads), F32),
        ((heads, tokens), F32),
        ((STATE, inner_local), F32),
        ((STATE, inner_local), F32),
        ((STATE, inner_local), F32),
        ((STATE, inner_local), F32),
        ((heads, tokens, tokens), BF16),
        ((heads, tokens, tokens), BF16),
        ((tokens, inner_local), F32),
        ((tokens, inner_local), BF16),
        ((tokens, inner_local), BF16),
        ((tokens, heads), F32),
        ((tokens, heads), F32),
        ((8, inner_local), F32),
        ((8, inner_local), F32),
        ((1, inner_local), F32),
        ((tokens, 128), F32),
        ((max(sizes[2] - 1, 1), tokens, 128), F32),
        ((peers, 1, inner_local), F32),
        ((8, 128), F32),
        ((peers, 8, 128), F32),
    ]
    seq, head_sum, gain_total = pl.pallas_call(
        functools.partial(trained, sizes),
        out_shape=(
            jax.ShapeDtypeStruct((tokens, inner_local), BF16),
            jax.ShapeDtypeStruct((8, 128), F32),
            jax.ShapeDtypeStruct((1, inner_local), F32),
        ),
        in_specs=[vmem, whole, vmem, vmem, whole] + [vmem] * 6,
        out_specs=(vmem,) * 3,
        scratch_shapes=[pltpu.VMEM(shape, kind) for shape, kind in scratch]
        + [dma((chunks * HOPS,))] * 4
        + [dma((max(sizes[2] - 1, 1),))] * 2
        + [dma((peers,))] * 4
        + [dma((2,))],
        compiler_params=pltpu.CompilerParams(
            collective_id=0, has_side_effects=True, vmem_limit_bytes=63 * 1024 * 1024
        ),
        name="trained",
    )(x, gates, b, c, cot, dt, dt.T, jax.nn.sigmoid(z), head_params, head_params.T, gain[None])
    return seq, head_sum[:3, :heads], gain_total[0]


def on_device(
    train_values,
    train_gates,
    train_writes,
    train_reads,
    train_steps,
    out_cotangent,
    head_params,
    norm_gain,
    slow_heads,
    slow_gain,
    roll_state,
    roll_values,
    roll_gates,
    roll_writes,
    roll_reads,
    roll_steps,
    roll_lengths,
):
    seq_out, head_sum, gain_total = train(
        train_values[0],
        train_gates[0],
        train_writes[0],
        train_reads[0],
        train_steps[0],
        out_cotangent[0],
        head_params,
        norm_gain,
    )
    heads = train_steps.shape[2]
    inner_local = train_values.shape[2]
    inner = inner_local * lax.axis_size("shd")
    blend_gain = KEEP_SHARE * slow_gain + (1.0 - KEEP_SHARE) * (norm_gain - STEP_RATE * gain_total)
    blend_heads = KEEP_SHARE * slow_heads + (1.0 - KEEP_SHARE) * (
        head_params - STEP_RATE * head_sum
    )
    rows = roll_state.shape[0]
    groups = roll_writes.shape[2] // STATE
    active = roll_lengths[:, None] > jnp.arange(STEPS)[None, :]
    steps = jnp.where(active[:, :, None], jax.nn.softplus(roll_steps + blend_heads[1]), 0.0)
    decay = -jnp.exp(blend_heads[0]) * steps
    sums = [decay[:, 0]]
    for k in range(1, STEPS):
        sums.append(sums[-1] + decay[:, k])
    x = roll_values.astype(F32).reshape(rows, STEPS, heads, HEAD_DIM)
    writes = roll_writes.reshape(rows, STEPS, groups, STATE)
    reads = roll_reads.reshape(rows, STEPS, groups, STATE)
    grouped = roll_state.reshape(rows, groups, heads // groups * HEAD_DIM, STATE)
    first = jnp.einsum("rkgn,rgqn->rkgq", reads, grouped, preferred_element_type=F32)
    first = first.reshape(rows, STEPS, heads, HEAD_DIM)
    cross = jnp.einsum("rkgn,rjgn->rkjg", reads, writes, preferred_element_type=F32)
    cross = jnp.repeat(cross, heads // groups, axis=3)
    wide_writes = expand_groups(roll_writes, heads).astype(F32)
    final = jnp.exp(sums[-1])[:, :, None, None] * roll_state.astype(F32)
    for j in range(STEPS):
        share = jnp.exp(sums[-1] - sums[j]) * steps[:, j]
        final = final + (share[:, :, None] * x[:, j])[..., None] * wide_writes[:, j, :, None, :]
    read = []
    for k in range(STEPS):
        now = jnp.exp(sums[k])[:, :, None] * first[:, k] + blend_heads[2][:, None] * x[:, k]
        for j in range(k + 1):
            share = jnp.exp(sums[k] - sums[j]) * steps[:, j] * cross[:, k, j]
            now = now + share[:, :, None] * x[:, j]
        read.append(now)
    gated = jnp.stack(read, axis=1).reshape(rows, STEPS, inner_local)
    gated = gated * jax.nn.silu(roll_gates.astype(F32))
    squares = lax.psum(jnp.sum(gated * gated, axis=2), "shd")
    shown = gated * lax.rsqrt(squares / inner + EPSILON)[..., None] * blend_gain
    roll_out = jnp.where(active[:, :, None], shown, 0.0).astype(BF16)
    return (seq_out[None], head_sum, gain_total, blend_heads, blend_gain, roll_out, final)


def solution(mesh):
    in_specs = (
        P("grp", "ctx", "shd"),
        P("grp", "ctx", "shd"),
        P("grp", "ctx", "shd"),
        P("grp", "ctx", "shd"),
        P("grp", "ctx", "shd"),
        P("grp", "ctx", "shd"),
        P(None, "shd"),
        P("shd"),
        P(None, "shd"),
        P("shd"),
        P(("grp", "ctx"), "shd", None, None),
        P(("grp", "ctx"), None, "shd"),
        P(("grp", "ctx"), None, "shd"),
        P(("grp", "ctx"), None, "shd"),
        P(("grp", "ctx"), None, "shd"),
        P(("grp", "ctx"), None, "shd"),
        P(("grp", "ctx")),
    )
    out_specs = (
        P("grp", "ctx", "shd"),
        P(None, "shd"),
        P("shd"),
        P(None, "shd"),
        P("shd"),
        P(("grp", "ctx"), None, "shd"),
        P(("grp", "ctx"), "shd", None, None),
    )
    return jax.shard_map(
        on_device, mesh=mesh, in_specs=in_specs, out_specs=out_specs, check_vma=False
    )
```
